32 devices in a mesh: row: 4 (over z), col: 8 (over y, x, core).
Axes of the slice: x: 2, y: 2, z: 4, core: 2. Of those that a mesh axis runs over, the one named last changes fastest.
Arguments:
- tokens: bfloat16 [192, 384, 256], P('row', 'col'), may hold values from -6 to 6
- registers: bfloat16 [64, 256], replicated, may hold values from -6 to 6
- tile_mask: int32 [24, 48], P('row', 'col'), may hold values 0 or 1
- w_qkv: bfloat16 [2, 256, 768], replicated, may hold values from -4 to 4
- w_out: bfloat16 [2, 256, 256], replicated, may hold values from -0.375 to 0.375
- w_up: bfloat16 [2, 256, 1024], replicated, may hold values from -0.375 to 0.375
- w_down: bfloat16 [2, 1024, 256], replicated, may hold values from -0.1875 to 0.1875
- norm_attn: float32 [2, 256], replicated, may hold values from 0.1 to 1.9
- norm_mlp: float32 [2, 256], replicated, may hold values from 0.1 to 1.9
Outputs:
- tokens_out: bfloat16 [192, 384, 256], P('row', 'col')
- registers_out: bfloat16 [64, 256], replicated
The draws below stay inside these ranges and needn't reach their ends.
All inputs are finite; a program needn't handle non-finite values. No bound on the sum of `tile_mask` on one device may be relied on, other than what follows from the above.
Results may differ from the reference program's by a relative error of at most 0.025.
Values may be sent and summed in bfloat16 or wider, within the bound.
No kernel may reach another device: no remote copies, remote signals or barrier semaphores. Data moves between devices by JAX's collectives and lax.ppermute only.
A program may use at most 128 MiB of HBM per device.

```python
import math
import jax
import jax.numpy as jnp
from jax import lax

D = 256
HEADS = 8
HID = 1024
REGS = 64
LAYERS = 2
RD = 48
CD = 48
NR = 192
NC = 384
N_ROW = 4
N_COL = 8


def draw_w_qkv(key, part):
    first = jax.random.fold_in(key, 0)
    base = jax.random.truncated_normal(first, -3.0, 3.0, (LAYERS, D, 3 * D), jnp.float32) / jnp.sqrt(jnp.float32(D))
    return base.astype(jnp.bfloat16)


def plant(result, rng, least, high):
    shape = result.shape
    index_at = [jax.random.randint(jax.random.fold_in(rng, axis), (), 0, shape[axis]) for axis in range(len(shape))]
    result = result.at[tuple(index_at)].set(least)
    longest = shape.index(max(shape))
    index_at[longest] = (index_at[longest] + 1) % shape[longest]
    return result.at[tuple(index_at)].set(high)


def levels(own_key, dims, cuts, smallest, high):
    level = 1.0
    for axis_at, shards_of in cuts:
        steps = jax.random.uniform(jax.random.fold_in(jax.random.fold_in(own_key, 6), axis_at), (shards_of,), jnp.float32, smallest / len(cuts), high / len(cuts))
        level = level * jnp.repeat(jnp.exp(steps), dims[axis_at] // shards_of).reshape((-1,) + (1,) * (len(dims) - 1 - axis_at))
    return level


def normal_values(own_key, dims, width, limit, cuts=(), kind=jnp.bfloat16):
    entries = width * jax.random.normal(own_key, dims, jnp.float32)
    if cuts:
        entries = entries * levels(own_key, dims, cuts, -0.22, 0.18)
    return jnp.clip(entries, -limit, limit).astype(kind)


def setup_inputs(seed: int = 0) -> dict:
    splits = jax.random.split(jax.random.key(seed), 10)
    return {
        "tokens": normal_values(splits[0], (NR, NC, D), 1.0, 6.0, ((0, 4), (1, 8))),
        "registers": normal_values(splits[1], (REGS, D), 1.0, 6.0),
        "tile_mask": plant((jax.random.randint(splits[2], (NR // 8, NC // 8), 0, 4) < 3).astype(jnp.int32), jax.random.fold_in(splits[2], 1), 0, 1),
        "w_qkv": draw_w_qkv(jax.random.fold_in(splits[9], 71), 0),
        "w_out": normal_values(splits[4], (LAYERS, D, D), D ** -0.5, 0.375),
        "w_up": normal_values(splits[5], (LAYERS, D, HID), D ** -0.5, 0.375),
        "w_down": normal_values(splits[6], (LAYERS, HID, D), HID ** -0.5, 0.1875),
        "norm_attn": jnp.clip(1.0 + 0.18 * jax.random.normal(splits[7], (LAYERS, D), jnp.float32), 0.1, 1.9),
        "norm_mlp": jnp.clip(1.0 + 0.18 * jax.random.normal(splits[8], (LAYERS, D), jnp.float32), 0.1, 1.9),
    }


neg_large = -1e+30
eps_norm = 1e-05
dilation_list = (1, 2)

def layer_norm(x, gain):
    value_rows = x.astype(jnp.float32)
    mean = lax.optimization_barrier(jnp.mean(value_rows, axis=-1, keepdims=True))
    centred = value_rows - mean
    spread = lax.optimization_barrier(jnp.mean(centred * centred, axis=-1, keepdims=True))
    return centred * lax.rsqrt(spread + eps_norm) * gain.astype(jnp.float32)

def window_table():
    query_rows = jnp.arange(64)
    key_rows = jnp.arange(576)
    qrow = (query_rows // 8)[:, None]
    qcol = (query_rows % 8)[:, None]
    krow = (key_rows // 24)[None, :]
    kcol = (key_rows % 24)[None, :]
    return (krow >= qrow) & (krow <= qrow + 12) & (kcol >= qcol) & (kcol <= qcol + 12)

def split_into_tiles(receptive_field, dilation_step):
    grid_rows, grid_columns = (receptive_field.shape[0], receptive_field.shape[1])
    extra_tokens = receptive_field.shape[2:]
    remaining_tokens = tuple(range(len(extra_tokens)))
    row_offset, column_offset = (grid_rows // dilation_step, grid_columns // dilation_step)
    shifted_grid = receptive_field.reshape((row_offset, dilation_step, column_offset, dilation_step) + extra_tokens)
    shifted_grid = jnp.transpose(shifted_grid, (1, 3, 0, 2) + tuple((4 + token_count for token_count in remaining_tokens)))
    shifted_grid = shifted_grid.reshape((dilation_step * dilation_step, row_offset // 8, 8, column_offset // 8, 8) + extra_tokens)
    shifted_grid = jnp.transpose(shifted_grid, (0, 1, 3, 2, 4) + tuple((5 + token_count for token_count in remaining_tokens)))
    return shifted_grid.reshape((dilation_step * dilation_step * (row_offset // 8) * (column_offset // 8), 64) + extra_tokens)

def untile_grid(grid_tiles, dilation_step, grid_rows, grid_columns):
    window_width = grid_tiles.shape[-1]
    row_offset, column_offset = (grid_rows // dilation_step, grid_columns // dilation_step)
    shifted_grid = grid_tiles.reshape(dilation_step, dilation_step, row_offset // 8, column_offset // 8, 8, 8, window_width)
    shifted_grid = jnp.transpose(shifted_grid, (2, 4, 0, 3, 5, 1, 6))
    return shifted_grid.reshape(grid_rows, grid_columns, window_width)

def split_into_regions(padded_grid, dilation_step, grid_rows, grid_columns):
    extra_tokens = padded_grid.shape[2:]
    remaining_tokens = tuple(range(len(extra_tokens)))
    padded_grid = jnp.pad(padded_grid, ((0, 4 * dilation_step), (0, 4 * dilation_step)) + tuple(((0, 0) for token_count in remaining_tokens)))
    row_padding, column_padding = (grid_rows // dilation_step + 16, grid_columns // dilation_step + 16)
    shifted_grid = padded_grid.reshape((row_padding, dilation_step, column_padding, dilation_step) + extra_tokens)
    shifted_grid = jnp.transpose(shifted_grid, (1, 3, 0, 2) + tuple((4 + token_count for token_count in remaining_tokens)))
    shifted_grid = shifted_grid.reshape((dilation_step * dilation_step, row_padding // 8, 8, column_padding // 8, 8) + extra_tokens)
    shifted_grid = jnp.transpose(shifted_grid, (0, 1, 3, 2, 4) + tuple((5 + token_count for token_count in remaining_tokens)))
    tile_rows, tile_columns = (grid_rows // dilation_step // 8, grid_columns // dilation_step // 8)
    stacked_outputs = jnp.stack([shifted_grid[:, a:a + tile_rows, b:b + tile_columns] for a in range(3) for b in range(3)], axis=3)
    stacked_outputs = stacked_outputs.reshape((dilation_step * dilation_step, tile_rows, tile_columns, 3, 3, 8, 8) + extra_tokens)
    stacked_outputs = jnp.transpose(stacked_outputs, (0, 1, 2, 3, 5, 4, 6) + tuple((7 + token_count for token_count in remaining_tokens)))
    return stacked_outputs.reshape((dilation_step * dilation_step * tile_rows * tile_columns, 576) + extra_tokens)

def tile_attention(query_rows, key_rows, value_rows, valid_mask, register_keys, register_values, table):
    group = query_rows.shape[0]
    window_width = query_rows.shape[-1]
    head = window_width // HEADS
    scale = head ** (-0.5)
    q4 = query_rows.reshape(group, 64, HEADS, head).astype(jnp.float32)
    k4 = key_rows.reshape(group, 576, HEADS, head).astype(jnp.float32)
    v4 = value_rows.reshape(group, 576, HEADS, head).astype(jnp.float32)
    rk4 = register_keys.reshape(-1, HEADS, head).astype(jnp.float32)
    rv4 = register_values.reshape(-1, HEADS, head).astype(jnp.float32)
    near = jnp.einsum('tqhe,tkhe->thqk', q4, k4) * scale
    allowed = table[None, None] & (valid_mask[:, None, None, :] > 0.5)
    near = jnp.where(allowed, near, neg_large)
    far = jnp.einsum('tqhe,rhe->thqr', q4, rk4) * scale
    top = jnp.maximum(lax.optimization_barrier(jnp.max(near, axis=-1)), lax.optimization_barrier(jnp.max(far, axis=-1)))
    near_w = jnp.exp(near - top[..., None])
    far_w = jnp.exp(far - top[..., None])
    total = lax.optimization_barrier(jnp.sum(near_w, axis=-1)) + lax.optimization_barrier(jnp.sum(far_w, axis=-1))
    near_b = near_w.astype(jnp.bfloat16).astype(jnp.float32)
    far_b = far_w.astype(jnp.bfloat16).astype(jnp.float32)
    out = jnp.einsum('thqk,tkhe->tqhe', near_b, v4) + jnp.einsum('thqr,rhe->tqhe', far_b, rv4)
    out = out / jnp.transpose(total, (0, 2, 1))[..., None]
    return out.reshape(group, 64, window_width).astype(jnp.bfloat16)

def gather_neighbour_block(query_rows, key_padded, value_padded, mask_padded, register_keys, register_values, dilation_step):
    grid_rows, grid_columns = (query_rows.shape[0], query_rows.shape[1])
    table = window_table()
    query_tiles = split_into_tiles(query_rows, dilation_step)
    key_tiles = split_into_regions(key_padded, dilation_step, grid_rows, grid_columns)
    value_tiles = split_into_regions(value_padded, dilation_step, grid_rows, grid_columns)
    mask_tiles = split_into_regions(mask_padded, dilation_step, grid_rows, grid_columns)
    count = query_tiles.shape[0]
    group = math.gcd(count, 8)

    def one(pieces):
        return tile_attention(pieces[0], pieces[1], pieces[2], pieces[3], register_keys, register_values, table)
    output_list = lax.map(one, (query_tiles.reshape((count // group, group) + query_tiles.shape[1:]), key_tiles.reshape((count // group, group) + key_tiles.shape[1:]), value_tiles.reshape((count // group, group) + value_tiles.shape[1:]), mask_tiles.reshape((count // group, group) + mask_tiles.shape[1:])))
    return untile_grid(output_list.reshape(query_tiles.shape), dilation_step, grid_rows, grid_columns)

def combine_stats(first, second):
    peak = jnp.maximum(first[0], second[0])
    fa = jnp.exp(first[0] - peak)
    fb = jnp.exp(second[0] - peak)
    head = first[2].shape[1] // HEADS
    return (peak, first[1] * fa + second[1] * fb, first[2] * jnp.repeat(fa, head, axis=1) + second[2] * jnp.repeat(fb, head, axis=1))

def register_partial(reg_q, key_rows, value_rows, live):
    count, window_width = key_rows.shape
    head = window_width // HEADS
    scale = head ** (-0.5)
    rq4 = reg_q.reshape(-1, HEADS, head).astype(jnp.float32)
    k4 = key_rows.reshape(count, HEADS, head).astype(jnp.float32)
    v4 = value_rows.reshape(count, HEADS, head).astype(jnp.float32)
    scores = jnp.einsum('rhe,nhe->rhn', rq4, k4) * scale
    alive = live[None, None, :] > 0.5
    scores = jnp.where(alive, scores, neg_large)
    top = lax.optimization_barrier(jnp.max(scores, axis=-1))
    weights = jnp.where(alive, jnp.exp(scores - top[..., None]), 0.0)
    total = lax.optimization_barrier(jnp.sum(weights, axis=-1))
    weights_b = weights.astype(jnp.bfloat16).astype(jnp.float32)
    numer = jnp.einsum('rhn,nhe->rhe', weights_b, v4)
    return (top, total, numer.reshape(-1, window_width))

def finish_registers(stats, reg_q, register_keys, register_values):
    top, total, numer = stats
    regs, window_width = reg_q.shape
    head = window_width // HEADS
    scale = head ** (-0.5)
    rq4 = reg_q.reshape(regs, HEADS, head).astype(jnp.float32)
    rk4 = register_keys.reshape(regs, HEADS, head).astype(jnp.float32)
    rv4 = register_values.reshape(regs, HEADS, head).astype(jnp.float32)
    own = jnp.einsum('rhe,she->rhs', rq4, rk4) * scale
    own_top = lax.optimization_barrier(jnp.max(own, axis=-1))
    own_w = jnp.exp(own - own_top[..., None])
    own_total = lax.optimization_barrier(jnp.sum(own_w, axis=-1))
    own_b = own_w.astype(jnp.bfloat16).astype(jnp.float32)
    own_numer = jnp.einsum('rhs,she->rhe', own_b, rv4)
    peak = jnp.maximum(top, own_top)
    keep = jnp.exp(top - peak)
    keep_own = jnp.exp(own_top - peak)
    total_all = total * keep + own_total * keep_own
    numer_all = numer.reshape(regs, HEADS, head) * keep[..., None] + own_numer * keep_own[..., None]
    return (numer_all / total_all[..., None]).reshape(regs, window_width).astype(jnp.bfloat16)

def neighbourhood_grid_attention(query_rows, key_rows, value_rows, valid_mask, register_keys, register_values, dilation_step):
    window_reach = 6 * dilation_step
    key_padded = jnp.pad(key_rows, ((window_reach, window_reach), (window_reach, window_reach), (0, 0)))
    value_padded = jnp.pad(value_rows, ((window_reach, window_reach), (window_reach, window_reach), (0, 0)))
    mask_padded = jnp.pad(valid_mask, ((window_reach, window_reach), (window_reach, window_reach)))

    def block(index):
        brow = (index // N_COL).astype(jnp.int32) * RD
        bcol = (index % N_COL).astype(jnp.int32) * CD
        zero = jnp.int32(0)
        query_block = lax.dynamic_slice(query_rows, (brow, bcol, zero), (RD, CD, D))
        key_block = lax.dynamic_slice(key_padded, (brow, bcol, zero), (RD + 2 * window_reach, CD + 2 * window_reach, D))
        value_block = lax.dynamic_slice(value_padded, (brow, bcol, zero), (RD + 2 * window_reach, CD + 2 * window_reach, D))
        mask_block = lax.dynamic_slice(mask_padded, (brow, bcol), (RD + 2 * window_reach, CD + 2 * window_reach))
        return gather_neighbour_block(query_block, key_block, value_block, mask_block, register_keys, register_values, dilation_step)
    output_list = lax.map(block, jnp.arange(N_ROW * N_COL, dtype=jnp.int32))
    output_list = output_list.reshape(N_ROW, N_COL, RD, CD, D)
    return jnp.transpose(output_list, (0, 2, 1, 3, 4)).reshape(NR, NC, D)

def register_attention(reg_q, register_keys, register_values, key_rows, value_rows, valid_mask):
    blocks = N_ROW * N_COL
    key_block = key_rows.reshape(N_ROW, RD, N_COL, CD, D).transpose(0, 2, 1, 3, 4).reshape(blocks, RD * CD, D)
    value_block = value_rows.reshape(N_ROW, RD, N_COL, CD, D).transpose(0, 2, 1, 3, 4).reshape(blocks, RD * CD, D)
    mask_block = valid_mask.reshape(N_ROW, RD, N_COL, CD).transpose(0, 2, 1, 3).reshape(blocks, RD * CD)
    start = (jnp.full((REGS, HEADS), neg_large, jnp.float32), jnp.zeros((REGS, HEADS), jnp.float32), jnp.zeros((REGS, D), jnp.float32))

    def step(carry, pieces):
        part = register_partial(reg_q, pieces[0], pieces[1], pieces[2])
        return (combine_stats(carry, part), None)
    stats, unused = lax.scan(step, start, (key_block, value_block, mask_block))
    return finish_registers(stats, reg_q, register_keys, register_values)

def reference(tokens, registers, tile_mask, w_qkv, w_out, w_up, w_down, norm_attn, norm_mlp):
    valid_mask = jnp.repeat(jnp.repeat(tile_mask, 8, axis=0), 8, axis=1).astype(jnp.bfloat16)
    x, g = (tokens, registers)
    for attention_layer in range(LAYERS):
        dilation_step = dilation_list[attention_layer % 2]
        h = layer_norm(x, norm_attn[attention_layer]).astype(jnp.bfloat16)
        hg = layer_norm(g, norm_attn[attention_layer]).astype(jnp.bfloat16)
        qkv = jnp.dot(h, w_qkv[attention_layer], preferred_element_type=jnp.float32).astype(jnp.bfloat16)
        rqkv = jnp.dot(hg, w_qkv[attention_layer], preferred_element_type=jnp.float32).astype(jnp.bfloat16)
        query_rows, key_rows, value_rows = (qkv[..., :D], qkv[..., D:2 * D], qkv[..., 2 * D:])
        reg_q, register_keys, register_values = (rqkv[:, :D], rqkv[:, D:2 * D], rqkv[:, 2 * D:])
        attended_output = neighbourhood_grid_attention(query_rows, key_rows, value_rows, valid_mask, register_keys, register_values, dilation_step)
        reg_att = register_attention(reg_q, register_keys, register_values, key_rows, value_rows, valid_mask)
        x = (x.astype(jnp.float32) + jnp.dot(attended_output, w_out[attention_layer], preferred_element_type=jnp.float32)).astype(jnp.bfloat16)
        g = (g.astype(jnp.float32) + jnp.dot(reg_att, w_out[attention_layer], preferred_element_type=jnp.float32)).astype(jnp.bfloat16)
        h2 = layer_norm(x, norm_mlp[attention_layer]).astype(jnp.bfloat16)
        hg2 = layer_norm(g, norm_mlp[attention_layer]).astype(jnp.bfloat16)
        inner = jax.nn.gelu(jnp.dot(h2, w_up[attention_layer], preferred_element_type=jnp.float32)).astype(jnp.bfloat16)
        inner_g = jax.nn.gelu(jnp.dot(hg2, w_up[attention_layer], preferred_element_type=jnp.float32)).astype(jnp.bfloat16)
        x = (x.astype(jnp.float32) + jnp.dot(inner, w_down[attention_layer], preferred_element_type=jnp.float32)).astype(jnp.bfloat16)
        g = (g.astype(jnp.float32) + jnp.dot(inner_g, w_down[attention_layer], preferred_element_type=jnp.float32)).astype(jnp.bfloat16)
    return (x, g)
```

```python
import functools
import math

import jax
import jax.numpy as jnp
from jax import lax
from jax.experimental import pallas as pl
from jax.experimental.pallas import tpu as pltpu
from jax.sharding import PartitionSpec as P

HEADS = 8
HEAD = 32
WIDTH = 256
REGS = 64
TILE = 8
LAYERS = 2
DILATIONS = (1, 2)
REACH = 6
QROWS = 4
KROWS = QROWS + 2 * REACH
KEYS = 3 * KROWS * TILE
QTILE = QROWS * TILE
CHUNK = 256
NEG = -1e30
EPS = 1e-05
SCALE = math.log2(math.e) * HEAD**-0.5
F32 = jnp.float32
BF16 = jnp.bfloat16
VMEM_LIMIT = 60 * 1024 * 1024


def mm(a, b):
    return lax.dot_general(a, b, (((1,), (0,)), ((), ())), preferred_element_type=F32)


def mm_nt(a, b):
    return lax.dot_general(a, b, (((1,), (1,)), ((), ())), preferred_element_type=F32)


def normed(x, gain):
    v = x.astype(F32)
    mean = jnp.mean(v, axis=-1, keepdims=True)
    centred = v - mean
    spread = jnp.mean(centred * centred, axis=-1, keepdims=True)
    return (centred * lax.rsqrt(spread + EPS) * gain).astype(BF16)


def iota(shape, dim):
    return lax.broadcasted_iota(jnp.int32, shape, dim)


def ones_where(cond):
    return jnp.where(cond, 1.0, 0.0).astype(BF16)


def head_mask(rows_per_head):
    shape = (HEADS * rows_per_head, WIDTH)
    return ones_where(iota(shape, 0) // rows_per_head == iota(shape, 1) // HEAD)


def spread_heads(q, mask):
    return jnp.concatenate([q] * HEADS, axis=0) * mask


def diagonal(part):
    lane = iota((HEAD, WIDTH), 1) // REGS
    out = jnp.zeros((HEAD, WIDTH), F32)
    for b in range(WIDTH // REGS):
        out = out + jnp.where(lane == b, part[b * HEAD : (b + 1) * HEAD, :], 0.0)
    return out


def mlp(x, h2, w_up, w_down):
    u = jax.nn.gelu(mm(h2, w_up), approximate=True).astype(BF16)
    return (x.astype(F32) + mm(u, w_down)).astype(BF16)


def stats_kernel(x_ref, g_ref, bias_ref, wq_ref, wk_ref, wvt_ref, gain_ref, out_ref, t_ref, vt_ref):
    chunks = x_ref.shape[0] // CHUNK
    gain = gain_ref[...]
    rq = mm(normed(g_ref[...], gain), wq_ref[...]).astype(BF16)
    rq_bd = spread_heads(rq, head_mask(REGS))

    def first(i, top):
        rows = pl.ds(pl.multiple_of(i * CHUNK, CHUNK), CHUNK)
        h = normed(x_ref[rows, :], gain)
        k = mm(h, wk_ref[...]).astype(BF16)
        vt_ref[i] = mm_nt(wvt_ref[...], h).astype(BF16)
        bias = bias_ref[rows, :].astype(F32)
        t = mm_nt(k, rq_bd) * SCALE + jnp.concatenate([bias] * 4, axis=1)
        t_ref[rows, :] = t
        return jnp.maximum(top, jnp.max(t, axis=0, keepdims=True))

    top = lax.fori_loop(0, chunks, first, jnp.full((1, 2 * WIDTH), 3 * NEG, F32))

    def second(i, carry):
        total, n0, n1 = carry
        rows = pl.ds(pl.multiple_of(i * CHUNK, CHUNK), CHUNK)
        w = jnp.exp2(t_ref[rows, :] - top)
        total = total + jnp.sum(w, axis=0, keepdims=True)
        wb = w.astype(BF16)
        vt = vt_ref[i]
        n0 = n0 + mm(vt[:128], wb[:, :WIDTH])
        n1 = n1 + mm(vt[128:], wb[:, WIDTH:])
        return total, n0, n1

    zero = jnp.zeros((128, WIDTH), F32)
    total, n0, n1 = lax.fori_loop(
        0, chunks, second, (jnp.zeros((1, 2 * WIDTH), F32), zero, zero)
    )
    out_ref[0:HEAD, :] = jnp.concatenate([diagonal(n0), diagonal(n1)], axis=1)
    rest = iota((8, 2 * WIDTH), 0)
    out_ref[HEAD : HEAD + 8, :] = jnp.where(rest == 0, top, jnp.where(rest == 1, total, 0.0))


def finish_kernel(
    stats_ref, g_ref, wq_ref, wk_ref, wvt_ref, gain_ref, wo_ref, wu_ref, wd_ref, gain2_ref, out_ref
):
    g = g_ref[...]
    hg = normed(g, gain_ref[...])
    rq = mm(hg, wq_ref[...]).astype(BF16)
    rk = mm(hg, wk_ref[...]).astype(BF16)
    rvt = mm_nt(wvt_ref[...], hg).astype(BF16)
    rq_bd = spread_heads(rq, head_mask(REGS))
    own = mm_nt(rk, rq_bd) * SCALE
    own_top = jnp.max(own, axis=0, keepdims=True)
    w = jnp.exp2(own - own_top)
    own_total = jnp.sum(w, axis=0, keepdims=True)
    wb = w.astype(BF16)
    own_numer = jnp.concatenate(
        [diagonal(mm(rvt[:128], wb[:, :WIDTH])), diagonal(mm(rvt[128:], wb[:, WIDTH:]))], axis=1
    )
    top = stats_ref[HEAD : HEAD + 1, :]
    total = stats_ref[HEAD + 1 : HEAD + 2, :]
    peak = jnp.maximum(top, own_top)
    keep = jnp.exp2(top - peak)
    keep_own = jnp.exp2(own_top - peak)
    total = total * keep + own_total * keep_own
    z = ((stats_ref[0:HEAD, :] * keep + own_numer * keep_own) / total).astype(BF16)
    shape = (WIDTH, HEADS * REGS)
    mask = ones_where(iota(shape, 0) // HEAD == iota(shape, 1) // REGS)
    z = jnp.concatenate([z] * HEADS, axis=0) * mask
    pick_shape = (REGS, HEADS * REGS)
    pick = ones_where(iota(pick_shape, 0) == iota(pick_shape, 1) % REGS)
    attended = mm_nt(pick, z).astype(BF16)
    g = (g.astype(F32) + mm(attended, wo_ref[...])).astype(BF16)
    out_ref[...] = mlp(g, normed(g, gain2_ref[...]), wu_ref[...], wd_ref[...])


def layer_kernel(
    x_ref, bias_ref, g_ref, wq_ref, wk_ref, wvt_ref, gain_ref, wo_ref, wu_ref, wd_ref, gain2_ref,
    out_ref, h_ref, k_ref, q_ref, vt_ref, win_ref, mask_ref, att_ref,
):
    grids, groups, key_rows, _ = x_ref.shape
    own_groups, rows = groups - 2, key_rows - 2 * REACH * TILE
    strips = rows // QTILE
    own = pl.ds(REACH * TILE, rows)
    gain = gain_ref[...]

    hg = normed(g_ref[...], gain)
    rk = mm(hg, wk_ref[...]).astype(BF16)
    rvt = mm_nt(wvt_ref[...], hg).astype(BF16)
    mask_ref[...] = head_mask(QTILE)
    shape = (KEYS, 128)
    key, query = iota(shape, 0), iota(shape, 1) % QTILE
    row_step = (key % (KROWS * TILE)) // TILE - query // TILE
    col_step = (key // (KROWS * TILE) - 1) * TILE + key % TILE - query % TILE
    near = (row_step >= 0) & (row_step <= 2 * REACH) & (col_step >= -REACH) & (col_step <= REACH)
    win_ref[...] = jnp.where(near, 0.0, NEG)

    def project(n, carry):
        gr, c = n // groups, n % groups
        h = normed(x_ref[gr, c], gain)
        h_ref[gr, c] = h
        k_ref[gr, c] = mm(h, wk_ref[...]).astype(BF16)
        return carry

    lax.fori_loop(0, grids * groups, project, 0)

    def queries(n, carry):
        gr, c = n // own_groups, n % own_groups
        q_ref[gr, c] = mm(h_ref[gr, c + 1, own, :], wq_ref[...]).astype(BF16)
        return carry

    lax.fori_loop(0, grids * own_groups, queries, 0)

    half = (128, 128)
    diag = iota(half, 0) // HEAD == iota(half, 1) // QTILE
    pick_shape = (QTILE, 128)
    pick = ones_where(iota(pick_shape, 0) == iota(pick_shape, 1) % QTILE)

    def strip(n, carry):
        gr, i = n // strips, n % strips
        start = pl.multiple_of(i * QTILE, QTILE)
        key_at = pl.ds(start, KROWS * TILE)
        hs = h_ref[gr, :, key_at, :].reshape(groups * KROWS * TILE, WIDTH)
        vt_ref[...] = mm_nt(wvt_ref[...], hs).astype(BF16)
        for j in range(own_groups):
            q = q_ref[gr, j, pl.ds(start, QTILE), :]
            q_bd = spread_heads(q, mask_ref[...])
            k = k_ref[gr, j : j + 3, key_at, :].reshape(KEYS, WIDTH)
            bias = bias_ref[gr, j : j + 3, key_at, :].reshape(KEYS, 128).astype(F32) + win_ref[...]
            s = mm_nt(jnp.concatenate([k, rk], axis=0), q_bd) * SCALE
            near_s = s[:KEYS] + jnp.concatenate([bias, bias], axis=1)
            far_s = s[KEYS:]
            top = jnp.maximum(
                jnp.max(near_s, axis=0, keepdims=True), jnp.max(far_s, axis=0, keepdims=True)
            )
            near_w = jnp.exp2(near_s - top)
            far_w = jnp.exp2(far_s - top)
            total = jnp.sum(near_w, axis=0, keepdims=True) + jnp.sum(far_w, axis=0, keepdims=True)
            w = jnp.concatenate([near_w.astype(BF16), far_w.astype(BF16)], axis=0)
            inverse = 1.0 / total
            lanes = slice(j * KROWS * TILE, j * KROWS * TILE + KEYS)
            parts = []
            for a in range(2):
                part = slice(128 * a, 128 * a + 128)
                vt = jnp.concatenate([vt_ref[part, lanes], rvt[part]], axis=1)
                o = mm(vt, w[:, part]) * inverse[:, part]
                parts.append(mm_nt(pick, jnp.where(diag, o, 0.0).astype(BF16)))
            att_ref[gr, j, pl.ds(start, QTILE), :] = jnp.concatenate(parts, axis=1).astype(BF16)
        return carry

    lax.fori_loop(0, grids * strips, strip, 0)

    def tail(n, carry):
        gr, c = n // own_groups, n % own_groups
        x = x_ref[gr, c + 1, own, :]
        x = (x.astype(F32) + mm(att_ref[gr, c], wo_ref[...])).astype(BF16)
        out_ref[gr, c] = mlp(x, normed(x, gain2_ref[...]), wu_ref[...], wd_ref[...])
        return carry

    lax.fori_loop(0, grids * own_groups, tail, 0)


def params():
    return pltpu.CompilerParams(vmem_limit_bytes=VMEM_LIMIT)


def register_stats(x, g, bias, w):
    tokens = x.shape[0]
    return pl.pallas_call(
        stats_kernel,
        out_shape=jax.ShapeDtypeStruct((HEAD + 8, HEADS * REGS), F32),
        scratch_shapes=[
            pltpu.VMEM((tokens, HEADS * REGS), F32),
            pltpu.VMEM((tokens // CHUNK, WIDTH, CHUNK), BF16),
        ],
        compiler_params=params(),
        name="register_stats",
    )(x, g, bias, w["q"], w["k"], w["vt"], w["gain"])


def finish_registers(stats, g, w):
    return pl.pallas_call(
        finish_kernel,
        out_shape=jax.ShapeDtypeStruct(g.shape, BF16),
        compiler_params=params(),
        name="finish_registers",
    )(
        stats, g, w["q"], w["k"], w["vt"], w["gain"], w["out"], w["up"], w["down"], w["gain2"]
    )


def token_layer(x, bias, g, w):
    grids, groups, key_rows, _ = x.shape
    own = (grids, groups - 2, key_rows - 2 * REACH * TILE, WIDTH)
    return pl.pallas_call(
        layer_kernel,
        out_shape=jax.ShapeDtypeStruct(own, BF16),
        scratch_shapes=[
            pltpu.VMEM(x.shape, BF16),
            pltpu.VMEM(x.shape, BF16),
            pltpu.VMEM(own, BF16),
            pltpu.VMEM((WIDTH, groups * KROWS * TILE), BF16),
            pltpu.VMEM((KEYS, 128), F32),
            pltpu.VMEM((HEADS * QTILE, WIDTH), BF16),
            pltpu.VMEM(own, BF16),
        ],
        compiler_params=params(),
        name="token_layer",
    )(
        x, bias, g, w["q"], w["k"], w["vt"], w["gain"], w["out"], w["up"], w["down"], w["gain2"]
    )


def combine(a, b):
    top_a, top_b = a[HEAD : HEAD + 1], b[HEAD : HEAD + 1]
    peak = jnp.maximum(top_a, top_b)
    fa, fb = jnp.exp2(top_a - peak), jnp.exp2(top_b - peak)
    out = a * fa + b * fb
    row = lax.broadcasted_iota(jnp.int32, out.shape, 0)
    return jnp.where(row == HEAD, peak, out)


def joined(stats):
    for axis in ("col", "row"):
        count = lax.axis_size(axis)
        step = 1
        while step < count:
            other = lax.ppermute(stats, axis, [(i, i ^ step) for i in range(count)])
            stats = combine(stats, other)
            step *= 2
    return stats


def extended(block, widths):
    for (axis, dim), width in zip((("row", 0), ("col", 1)), widths):
        count = lax.axis_size(axis)
        forward = [(i, i + 1) for i in range(count - 1)]
        backward = [(target, source) for source, target in forward]
        size = block.shape[dim]
        low = lax.ppermute(
            lax.slice_in_dim(block, size - width, size, axis=dim), axis, forward
        )
        high = lax.ppermute(lax.slice_in_dim(block, 0, width, axis=dim), axis, backward)
        block = jnp.concatenate([low, block, high], axis=dim)
    return block


def to_groups(x, dil):
    rows, cols = x.shape[:2]
    rest = x.shape[2:]
    x = x.reshape((rows // dil, dil, cols // (dil * TILE), TILE, dil) + rest)
    x = jnp.transpose(x, (1, 4, 2, 0, 3) + tuple(range(5, x.ndim)))
    return x.reshape((dil * dil, cols // (dil * TILE), rows // dil * TILE) + rest)


def from_groups(x, dil, rows, cols):
    x = x.reshape(dil, dil, cols // (dil * TILE), rows // dil, TILE, WIDTH)
    return jnp.transpose(x, (3, 0, 2, 4, 1, 5)).reshape(rows, cols, WIDTH)


def layer_weights(l, w_qkv, w_out, w_up, w_down, norm_attn, norm_mlp):
    return {
        "q": w_qkv[l, :, :WIDTH],
        "k": w_qkv[l, :, WIDTH : 2 * WIDTH],
        "vt": w_qkv[l, :, 2 * WIDTH :].T,
        "out": w_out[l],
        "up": w_up[l],
        "down": w_down[l],
        "gain": norm_attn[l : l + 1],
        "gain2": norm_mlp[l : l + 1],
    }


def shards(tokens, registers, tile_mask, w_qkv, w_out, w_up, w_down, norm_attn, norm_mlp):
    rows, cols, _ = tokens.shape
    tiles = extended(tile_mask.astype(BF16), (2, 2))
    x, g = tokens, registers
    for l in range(LAYERS):
        dil = DILATIONS[l % 2]
        w = layer_weights(l, w_qkv, w_out, w_up, w_down, norm_attn, norm_mlp)
        row_halo, col_halo = REACH * dil, TILE * dil
        valid = jnp.repeat(jnp.repeat(tiles, TILE, axis=0), TILE, axis=1)
        valid = valid[
            2 * TILE - row_halo : 2 * TILE + rows + row_halo,
            2 * TILE - col_halo : 2 * TILE + cols + col_halo,
        ]
        bias = jnp.where(to_groups(valid, dil) > 0.5, 0.0, NEG).astype(BF16)
        bias = jnp.broadcast_to(bias[..., None], bias.shape + (128,))
        own_rows = rows // dil * TILE
        bias_own = bias[:, 1:-1, REACH * TILE : REACH * TILE + own_rows].reshape(-1, 128)
        x_own = to_groups(x, dil).reshape(-1, WIDTH)
        stats = joined(register_stats(x_own, g, bias_own, w))
        keys = to_groups(extended(x, (row_halo, col_halo)), dil)
        x = from_groups(token_layer(keys, bias, g, w), dil, rows, cols)
        g = finish_registers(stats, g, w)
    return x, g


def solution(mesh):
    return jax.shard_map(
        shards,
        mesh=mesh,
        in_specs=(P("row", "col", None), P(), P("row", "col"), P(), P(), P(), P(), P(), P()),
        out_specs=(P("row", "col", None), P()),
        check_vma=False,
    )
```

```python
import math

import jax
import jax.numpy as jnp
from jax import lax
from jax.experimental import pallas as pl
from jax.experimental.pallas import tpu as pltpu
from jax.sharding import PartitionSpec as P

HEADS = 8
HEAD = 32
WIDTH = 256
REGS = 64
TILE = 8
LAYERS = 2
DILATIONS = (1, 2)
REACH = 6
QROWS = 4
KROWS = QROWS + 2 * REACH
GKEYS = KROWS * TILE
KEYS = 3 * GKEYS
QTILE = QROWS * TILE
RIM = REACH * TILE
CHUNK = 384
ONES = 16
UNITS = 8
NEG = -1e30
BIG = 1e30
LIMIT = 2.0**100
EPS = 1e-05
SCALE = math.log2(math.e) * HEAD**-0.5
F32 = jnp.float32
BF16 = jnp.bfloat16


def mm(a, b):
    return lax.dot_general(a, b, (((1,), (0,)), ((), ())), preferred_element_type=F32)


def mm_nt(a, b):
    return lax.dot_general(a, b, (((1,), (1,)), ((), ())), preferred_element_type=F32)


def normed(x, gain):
    v = x.astype(F32)
    mean = jnp.mean(v, axis=-1, keepdims=True)
    centred = v - mean
    spread = jnp.mean(centred * centred, axis=-1, keepdims=True)
    return centred * lax.rsqrt(spread + EPS) * gain


def iota(shape, dim):
    return lax.broadcasted_iota(jnp.int32, shape, dim)


def ones_where(cond):
    return jnp.where(cond, 1.0, 0.0).astype(BF16)


def head_mask(rows_per_head):
    shape = (HEADS * rows_per_head, WIDTH)
    return ones_where(iota(shape, 0) // rows_per_head == iota(shape, 1) // HEAD)


def spread_heads(q, mask):
    return jnp.concatenate([q] * HEADS, axis=0) * mask


def twice(a):
    return jnp.concatenate([a, a], axis=1)


def first_lane():
    return ones_where(iota((ONES, 128), 1) == 0)


def diagonal(part):
    lane = iota((HEAD, WIDTH), 1) // REGS
    out = jnp.zeros((HEAD, WIDTH), F32)
    for b in range(WIDTH // REGS):
        out = out + jnp.where(lane == b, part[b * HEAD : (b + 1) * HEAD, :], 0.0)
    return out


def mlp(x, gain2, w_up, w_down):
    z = mm(normed(x, gain2).astype(BF16), w_up)
    slope = math.sqrt(2.0 / math.pi)
    u = (z + z * jnp.tanh(z * (slope + (slope * 0.044715) * (z * z)))).astype(BF16)
    return (x.astype(F32) + 0.5 * mm(u, w_down)).astype(BF16)


def block_valid(mask_ref, dil, group):
    rows = TILE * TILE // dil
    shape = (rows, 128)
    parts = []
    for r in range(mask_ref.shape[0]):
        if dil == 1:
            part = jnp.full(shape, mask_ref[r, group].astype(F32), F32)
        else:
            low = jnp.full(shape, mask_ref[r, 2 * group].astype(F32), F32)
            high = jnp.full(shape, mask_ref[r, 2 * group + 1].astype(F32), F32)
            part = jnp.where(iota(shape, 0) % TILE < TILE // 2, low, high)
        parts.append(part)
    return jnp.concatenate(parts, axis=0)


def own_kernel(
    dil, groups, x_ref, mask_ref, g_ref, wq_ref, wk_ref, wvt_ref, gain_ref,
    h_ref, k_ref, q_ref, v_ref, stats_ref, left_ref, right_ref, acc_ref, t_ref,
):
    gain = gain_ref[...]
    chunks = x_ref.shape[0] // CHUNK
    per_chunk = dil * dil * groups // chunks
    hg = normed(g_ref[...], gain).astype(BF16)
    rq_bd = spread_heads((mm(hg, wq_ref[...]) * SCALE).astype(BF16), head_mask(REGS))
    rk = mm(hg, wk_ref[...]).astype(BF16)
    shift = jnp.max(mm_nt(rk, rq_bd), axis=0, keepdims=True)
    lane = first_lane()
    acc_ref[...] = jnp.zeros_like(acc_ref)

    def accumulate(h, valid, w):
        vt = mm_nt(wvt_ref[...], h).astype(BF16)
        ones = mm_nt(lane, valid).astype(BF16)
        for a in range(2):
            lhs = jnp.concatenate([vt[128 * a : 128 * a + 128], ones], axis=0)
            acc_ref[a] += mm(lhs, w[:, WIDTH * a : WIDTH * (a + 1)])

    def chunk(n, carry):
        rows = pl.ds(pl.multiple_of(n * CHUNK, CHUNK), CHUNK)
        valid = jnp.concatenate(
            [
                block_valid(mask_ref, dil, lax.rem(n * per_chunk + p, groups))
                for p in range(per_chunk)
            ],
            axis=0,
        )
        h32 = normed(x_ref[rows, :], gain)
        q_ref[rows, :] = (mm(h32.astype(BF16), wq_ref[...]) * SCALE).astype(BF16)
        h = (h32 * twice(valid)).astype(BF16)
        valid = valid.astype(BF16)
        k = mm(h, wk_ref[...]).astype(BF16)
        h_ref[rows, :] = h
        k_ref[rows, :] = k
        v_ref[rows, :] = valid
        accumulate(h, valid, jnp.exp2(mm_nt(k, rq_bd) - shift).astype(BF16))
        return carry

    lax.fori_loop(0, chunks, chunk, 0, unroll=2)

    size = left_ref.shape[1]
    for gr in range(dil * dil):
        for ref, c in ((left_ref, 0), (right_ref, groups - 1)):
            rows = slice((gr * groups + c) * size, (gr * groups + c + 1) * size)
            live = twice(v_ref[rows, :].astype(F32)) > 0.5
            ref[gr] = jnp.where(live, x_ref[rows, :].astype(F32), BIG).astype(BF16)

    def write(top):
        n0, n1 = acc_ref[0], acc_ref[1]
        stats_ref[0:HEAD, :] = jnp.concatenate([diagonal(n0), diagonal(n1)], axis=1)
        total = jnp.concatenate([n0[128:136], n1[128:136]], axis=1)
        row = iota((8, 2 * WIDTH), 0)
        stats_ref[HEAD : HEAD + 8, :] = jnp.where(row == 0, top, jnp.where(row == 1, total, 0.0))

    write(shift)
    worst = jnp.max(jnp.where(acc_ref[:, 128:136, :] < LIMIT, 0.0, 1.0))

    @pl.when(worst > 0.5)
    def _():
        def scores(n, top):
            rows = pl.ds(pl.multiple_of(n * CHUNK, CHUNK), CHUNK)
            live = jnp.concatenate([v_ref[rows, :].astype(F32)] * 4, axis=1) > 0.5
            t = jnp.where(live, mm_nt(k_ref[rows, :], rq_bd), NEG)
            t_ref[rows, :] = t
            return jnp.maximum(top, jnp.max(t, axis=0, keepdims=True))

        top = lax.fori_loop(0, chunks, scores, jnp.full((1, 2 * WIDTH), NEG, F32))
        acc_ref[...] = jnp.zeros_like(acc_ref)

        def weigh(n, carry):
            rows = pl.ds(pl.multiple_of(n * CHUNK, CHUNK), CHUNK)
            w = jnp.exp2(t_ref[rows, :] - top).astype(BF16)
            accumulate(h_ref[rows, :], v_ref[rows, :], w)
            return carry

        lax.fori_loop(0, chunks, weigh, 0)
        write(top)


def finish_kernel(
    stats_ref, g_ref, wq_ref, wk_ref, wvt_ref, gain_ref, wo_ref, wu_ref, wd_ref, gain2_ref, out_ref
):
    g = g_ref[...]
    hg = normed(g, gain_ref[...]).astype(BF16)
    rq_bd = spread_heads((mm(hg, wq_ref[...]) * SCALE).astype(BF16), head_mask(REGS))
    rk = mm(hg, wk_ref[...]).astype(BF16)
    rvt = mm_nt(wvt_ref[...], hg).astype(BF16)
    own = mm_nt(rk, rq_bd)
    own_top = jnp.max(own, axis=0, keepdims=True)
    w = jnp.exp2(own - own_top)
    own_total = jnp.sum(w, axis=0, keepdims=True)
    wb = w.astype(BF16)
    own_numer = jnp.concatenate(
        [diagonal(mm(rvt[:128], wb[:, :WIDTH])), diagonal(mm(rvt[128:], wb[:, WIDTH:]))], axis=1
    )
    top = stats_ref[HEAD : HEAD + 1, :]
    total = stats_ref[HEAD + 1 : HEAD + 2, :]
    peak = jnp.maximum(top, own_top)
    keep = jnp.exp2(top - peak)
    keep_own = jnp.exp2(own_top - peak)
    total = total * keep + own_total * keep_own
    z = ((stats_ref[0:HEAD, :] * keep + own_numer * keep_own) / total).astype(BF16)
    shape = (WIDTH, HEADS * REGS)
    mask = ones_where(iota(shape, 0) // HEAD == iota(shape, 1) // REGS)
    z = jnp.concatenate([z] * HEADS, axis=0) * mask
    pick_shape = (REGS, HEADS * REGS)
    pick = ones_where(iota(pick_shape, 0) == iota(pick_shape, 1) % REGS)
    attended = mm_nt(pick, z).astype(BF16)
    g = (g.astype(F32) + mm(attended, wo_ref[...])).astype(BF16)
    out_ref[...] = mlp(g, gain2_ref[...], wu_ref[...], wd_ref[...])


def attend_kernel(dil, edges, *refs):
    (
        flags_ref, mask_in_ref, x_ref, h_ref, k_ref, q_ref, v_ref, top_ref, bottom_ref, g_ref,
        wk_ref, wvt_ref, gain_ref, wo_ref, wu_ref, wd_ref, gain2_ref,
    ) = refs[:17]
    refs = refs[17:]
    grids, own_groups, rows, _ = x_ref.shape
    strips = rows // QTILE
    if edges:
        left_ref, right_ref, middle_ref = refs[:3]
        outs, refs = (refs[3:6], refs[6:]) if dil == 1 else (refs[3:4], refs[4:])
        new_ref, refs = refs[0], refs[1:]
        sources = [None, 0, 1, own_groups - 2, own_groups - 1, None]
        tiles, tile_step, own_at, own_step = 2, 3, 0, own_groups - 1
    else:
        new_ref, refs = refs[0], refs[1:]
        sources = list(range(own_groups))
        tiles, tile_step, own_at, own_step = own_groups - 2, 1, 1, 1
    kh_ref, kk_ref, kv_ref, vt_ref, win_ref, head_ref, att_ref, chk_ref, w_ref, o_ref = refs
    at_once = vt_ref.shape[0] // grids
    groups = len(sources)
    gain = gain_ref[...]
    lane = first_lane()

    hg = normed(g_ref[...], gain).astype(BF16)
    rk = mm(hg, wk_ref[...]).astype(BF16)
    rvt = mm_nt(wvt_ref[...], hg).astype(BF16)
    ones = jnp.full((ONES, REGS), 1.0, BF16)
    rvts = [jnp.concatenate([rvt[128 * a : 128 * a + 128], ones], axis=0) for a in range(2)]
    head_ref[...] = head_mask(QTILE)
    shape = (KEYS, 128)
    key, query = iota(shape, 0), iota(shape, 1) % QTILE
    row_step = (key % GKEYS) // TILE - query // TILE
    col_step = (key // GKEYS - 1) * TILE + key % TILE - query % TILE
    win_ref[...] = ones_where(
        (row_step >= 0) & (row_step <= 2 * REACH) & (col_step >= -REACH) & (col_step <= REACH)
    )
    chk_ref[...] = jnp.zeros_like(chk_ref)

    has = [flags_ref[0, n].astype(F32) for n in range(4)]

    def from_rim(x, known):
        x = x.astype(F32)
        valid = jnp.where(jnp.abs(x[:, 0:1]) < 0.5 * BIG, 1.0, 0.0) * known
        h = (normed(jnp.where(valid > 0.5, x, 0.0), gain) * valid).astype(BF16)
        k = mm(h, wk_ref[...]).astype(BF16)
        return h, k, jnp.broadcast_to(valid, (x.shape[0], 128)).astype(BF16)

    held = [(c, source) for c, source in enumerate(sources) if source is not None]

    def assemble(gr, carry):
        for c, source in held:
            for ref, own in ((kh_ref, h_ref), (kk_ref, k_ref), (kv_ref, v_ref)):
                ref[gr, c, RIM : RIM + rows, :] = own[gr, source]
        x = [top_ref[gr, source] for _, source in held]
        x += [bottom_ref[gr, source] for _, source in held]
        size = len(held) * RIM
        known = jnp.where(iota((2 * size, 1), 0) < size, has[0], has[1])
        parts = from_rim(jnp.concatenate(x, axis=0), known)
        for n, (c, _) in enumerate(held):
            for ref, part in zip((kh_ref, kk_ref, kv_ref), parts):
                ref[gr, c, 0:RIM, :] = part[n * RIM : (n + 1) * RIM]
                ref[gr, c, RIM + rows :, :] = part[size + n * RIM : size + (n + 1) * RIM]
        if edges:
            size = rows + 2 * RIM
            row = iota((size, 1), 0)
            rim = jnp.where(row < RIM, has[0], jnp.where(row < RIM + rows, 1.0, has[1]))
            known = jnp.concatenate([rim * has[2], rim * has[3]], axis=0)
            parts = from_rim(jnp.concatenate([left_ref[gr], right_ref[gr]], axis=0), known)
            for n, c in ((0, 0), (1, groups - 1)):
                for ref, part in zip((kh_ref, kk_ref, kv_ref), parts):
                    ref[gr, c] = part[n * size : (n + 1) * size]
        return carry

    lax.fori_loop(0, grids, assemble, 0, unroll=min(grids, 2))

    half = (128, 128)
    diag = iota(half, 0) // HEAD == iota(half, 1) // QTILE
    pick_shape = (QTILE, 128)
    pick = ones_where(iota(pick_shape, 0) == iota(pick_shape, 1) % QTILE)

    def keys_of(i):
        start = pl.multiple_of(i * QTILE, QTILE)
        return pl.ds(start, QTILE), pl.ds(start, GKEYS)

    def values(slot, gr, i):
        _, key_at = keys_of(i)
        hs = kh_ref[gr, :, key_at, :].reshape(groups * GKEYS, WIDTH)
        vs = kv_ref[gr, :, key_at, :].reshape(groups * GKEYS, 128)
        vt_ref[slot, 0:WIDTH, :] = mm_nt(wvt_ref[...], hs).astype(BF16)
        vt_ref[slot, WIDTH:, :] = mm_nt(lane, vs).astype(BF16)

    def scores(gr, i, t):
        query_at, key_at = keys_of(i)
        q_bd = spread_heads(q_ref[gr, own_at + t * own_step, query_at, :], head_ref[...])
        k = kk_ref[gr, pl.ds(t * tile_step, 3), key_at, :].reshape(KEYS, WIDTH)
        return mm_nt(jnp.concatenate([rk, k], axis=0), q_bd)

    def weighted(u, slot, t):
        lanes = pl.ds(t * tile_step * GKEYS, KEYS)
        if not isinstance(t, int):
            lanes = pl.ds(pl.multiple_of(t * tile_step * GKEYS, GKEYS), KEYS)
        totals = []
        for a in range(2):
            vt = jnp.concatenate(
                [vt_ref[slot, 128 * a : 128 * a + 128, lanes], vt_ref[slot, WIDTH:, lanes]], axis=0
            )
            o = mm(
                jnp.concatenate([vt, rvts[a]], axis=1), w_ref[u, :, 128 * a : 128 * a + 128]
            )
            total = o[128:129]
            totals.append(total)
            o_ref[u, a] = jnp.where(diag, o[:128] * (1.0 / total), 0.0).astype(BF16)
        return jnp.concatenate(totals, axis=1)

    def turned(u, gr, i, t):
        query_at, _ = keys_of(i)
        parts = [mm_nt(pick, o_ref[u, a]) for a in range(2)]
        att_ref[gr, t, query_at, :] = jnp.concatenate(parts, axis=1).astype(BF16)

    def batch(n, carry):
        slots = [(gr, n * at_once + i) for i in range(at_once) for gr in range(grids)]
        units = [(slot, t) for slot in range(len(slots)) for t in range(tiles)]
        bad = jnp.zeros((1, WIDTH), F32)
        for step in range(len(units) + 2):
            if step < len(units):
                slot, t = units[step]
                if t == 0:
                    values(slot, *slots[slot])
                s = scores(*slots[slot], t)
                shift = jnp.max(s[:REGS], axis=0, keepdims=True)
                w = jnp.exp2(s - shift).astype(BF16)
                w_ref[step, KEYS:, :] = w[:REGS]
                w_ref[step, :KEYS, :] = w[REGS:] * twice(win_ref[...])
            if 0 <= step - 1 < len(units):
                slot, t = units[step - 1]
                total = weighted(step - 1, slot, t)
                bad = jnp.maximum(bad, jnp.where(total < LIMIT, 0.0, 1.0))
            if step >= 2:
                slot, t = units[step - 2]
                turned(step - 2, *slots[slot], t)
        chk_ref[0:1, :] = jnp.maximum(chk_ref[0:1, :], bad)
        return carry

    lax.fori_loop(0, strips // at_once, batch, 0)

    @pl.when(jnp.max(chk_ref[...]) > 0.5)
    def _():
        def again(n, carry):
            gr, i = n // strips, n % strips
            _, key_at = keys_of(i)
            values(0, gr, i)

            def tile(t, carry):
                s = scores(gr, i, t)
                valid = kv_ref[gr, pl.ds(t * tile_step, 3), key_at, :].reshape(KEYS, 128)
                live = twice((valid * win_ref[...]).astype(F32)) > 0.5
                live = jnp.concatenate([jnp.full((REGS, WIDTH), True), live], axis=0)
                s = jnp.where(live, s, NEG)
                top = jnp.max(s, axis=0, keepdims=True)
                w = jnp.where(live, jnp.exp2(s - top), 0.0).astype(BF16)
                w_ref[0, KEYS:, :] = w[:REGS]
                w_ref[0, :KEYS, :] = w[REGS:]
                weighted(0, 0, t)
                turned(0, gr, i, t)
                return carry

            return lax.fori_loop(0, tiles, tile, carry)

        lax.fori_loop(0, grids * strips, again, 0)

    def tail(n, carry):
        gr, t = n // tiles, n % tiles
        x = x_ref[gr, own_at + t * own_step]
        x = (x.astype(F32) + mm(att_ref[gr, t], wo_ref[...])).astype(BF16)
        new_ref[gr, t] = mlp(x, gain2_ref[...], wu_ref[...], wd_ref[...])
        return carry

    lax.fori_loop(0, grids * tiles, tail, 0, unroll=2)
    if not edges:
        return

    def group(gr, c, at):
        if c == 0:
            return new_ref[gr, 0, at, :]
        if c == own_groups - 1:
            return new_ref[gr, 1, at, :]
        return middle_ref[gr, c - 1, at, :]

    square = (128, 128)
    to, of = iota(square, 0), iota(square, 1)
    if dil == 1:
        out_ref, first_ref, last_ref = outs
        a, b = to // 64, (to // 32) % 2
        rr, cc = (to % 32) // TILE, to % TILE
        source = (cc // 4) * 64 + (2 * rr + a) * TILE + 2 * (cc % 4) + b
        perm = ones_where(of == source)
        for c in range(own_groups // 2):
            for r in range(rows // 64):
                at = slice(64 * r, 64 * r + 64)
                both = jnp.concatenate([group(0, 2 * c, at), group(0, 2 * c + 1, at)], axis=0)
                y = mm(perm, both).astype(BF16)
                for gr in range(4):
                    out_ref[gr, c, 32 * r : 32 * r + 32, :] = y[32 * gr : 32 * gr + 32]
            live = twice(block_valid(mask_in_ref, 2, c)) > 0.5
            size = live.shape[0]
            for gr in range(4):
                for ref, at in ((first_ref, slice(0, RIM)), (last_ref, slice(size - RIM, size))):
                    y = jnp.where(live[at], out_ref[gr, c, at, :].astype(F32), BIG)
                    ref[gr, c] = y.astype(BF16)
    else:
        (out_ref,) = outs
        r, col = to // 16, to % 16
        source = (2 * (r % 2) + col % 2) * 32 + (r // 2) * TILE + col // 2
        perm = ones_where(of == source)
        for c in range(own_groups):
            for r in range(rows // 32):
                at = slice(32 * r, 32 * r + 32)
                four = jnp.concatenate([group(gr, c, at) for gr in range(4)], axis=0)
                y = mm(perm, four).astype(BF16)
                for n in range(TILE):
                    out_ref[TILE * r + n, 16 * c : 16 * c + 16, :] = y[16 * n : 16 * n + 16]


VMEM = pl.BlockSpec(memory_space=pltpu.VMEM)
SMEM = pl.BlockSpec(memory_space=pltpu.SMEM)


def call(kernel, name, out_shape, scratch, specs, micros, *args):
    return pl.pallas_call(
        kernel,
        out_shape=out_shape,
        in_specs=specs,
        out_specs=jax.tree.map(lambda _: VMEM, out_shape),
        scratch_shapes=scratch,
        compiler_params=pltpu.CompilerParams(vmem_limit_bytes=40 * 1024 * 1024),
        cost_estimate=pl.CostEstimate(
            flops=micros * 10**9, transcendentals=0, bytes_accessed=micros * 10**6
        ),
        name=name,
    )(*args)


def shape(dims, dtype=BF16):
    return jax.ShapeDtypeStruct(dims, dtype)


def own_tokens(dil, x, mask, g, w):
    grids, groups, rows, _ = x.shape
    tokens = grids * groups * rows
    outs = call(
        lambda *refs: own_kernel(dil, groups, *refs),
        "own_tokens",
        [
            shape((tokens, WIDTH)),
            shape((tokens, WIDTH)),
            shape((tokens, WIDTH)),
            shape((tokens, 128)),
            shape((HEAD + 8, HEADS * REGS), F32),
            shape((grids, rows, WIDTH)),
            shape((grids, rows, WIDTH)),
        ],
        [
            pltpu.VMEM((2, 128 + ONES, WIDTH), F32),
            pltpu.VMEM((tokens, HEADS * REGS), F32),
        ],
        [VMEM, SMEM] + [VMEM] * 5,
        6,
        x.reshape(tokens, WIDTH), mask, g, w["q"], w["k"], w["vt"], w["gain"],
    )
    split = [a.reshape(grids, groups, rows, a.shape[-1]) for a in outs[:4]]
    return split, outs[4], outs[5], outs[6]


def finish_registers(stats, g, w):
    return call(
        finish_kernel, "finish_registers", shape(g.shape), [], [VMEM] * 10, 3,
        stats, g, w["q"], w["k"], w["vt"], w["gain"], w["out"], w["up"], w["down"], w["gain2"],
    )


def attend(dil, flags, mask, x, own, rims, g, w, sides=None):
    grids, groups, rows, _ = x.shape
    h, k, q, v = own
    edges = sides is not None
    tiles = 2 if edges else groups - 2
    held = 6 if edges else groups
    at_once = max(1, UNITS // (grids * tiles))
    new = (grids, tiles, rows, WIDTH)
    keys = (grids, held, rows + 2 * RIM)
    scratch = [
        pltpu.VMEM(keys + (WIDTH,), BF16),
        pltpu.VMEM(keys + (WIDTH,), BF16),
        pltpu.VMEM(keys + (128,), BF16),
        pltpu.VMEM((at_once * grids, WIDTH + ONES, held * GKEYS), BF16),
        pltpu.VMEM((KEYS, 128), BF16),
        pltpu.VMEM((HEADS * QTILE, WIDTH), BF16),
        pltpu.VMEM(new, BF16),
        pltpu.VMEM((8, WIDTH), F32),
        pltpu.VMEM((at_once * grids * tiles, KEYS + REGS, WIDTH), BF16),
        pltpu.VMEM((at_once * grids * tiles, 2, 128, 128), BF16),
    ]
    if not edges:
        out = shape(new)
    else:
        scratch = [pltpu.VMEM(new, BF16)] + scratch
        if dil == 1:
            after = (4, groups // 2, rows // 2)
            rim = (4, groups // 2, RIM, WIDTH)
            out = [shape(after + (WIDTH,)), shape(rim), shape(rim)]
        else:
            out = [shape((mask.shape[0] * TILE, mask.shape[1] * TILE, WIDTH))]
    args = (
        flags, mask, x, h, k, q, v, *rims, g,
        w["k"], w["vt"], w["gain"], w["out"], w["up"], w["down"], w["gain2"],
    ) + (tuple(sides) if edges else ())
    return call(
        lambda *refs: attend_kernel(dil, edges, *refs),
        "attend_edges" if edges else "attend_middle",
        out,
        scratch,
        [SMEM, SMEM] + [VMEM] * (len(args) - 2),
        12,
        *args,
    )


def combine(a, b):
    top_a, top_b = a[HEAD : HEAD + 1], b[HEAD : HEAD + 1]
    peak = jnp.maximum(top_a, top_b)
    fa, fb = jnp.exp2(top_a - peak), jnp.exp2(top_b - peak)
    out = a * fa + b * fb
    row = lax.broadcasted_iota(jnp.int32, out.shape, 0)
    return jnp.where(row == HEAD, peak, out)


def joined(stats):
    for axis in ("col", "row"):
        count = lax.axis_size(axis)
        step = 1
        while step < count:
            other = lax.ppermute(stats, axis, [(i, i ^ step) for i in range(count)])
            stats = combine(stats, other)
            step *= 2
    return stats


def exchanged(first, last, axis):
    count = lax.axis_size(axis)
    forward = [(i, i + 1) for i in range(count - 1)]
    backward = [(target, source) for source, target in forward]
    return lax.ppermute(last, axis, forward), lax.ppermute(first, axis, backward)


def to_groups(x):
    rows, cols = x.shape[:2]
    x = jnp.transpose(x.reshape(rows, cols // TILE, TILE, WIDTH), (1, 0, 2, 3))
    return x.reshape(1, cols // TILE, rows * TILE, WIDTH)


def layer_weights(l, w_qkv, w_out, w_up, w_down, norm_attn, norm_mlp):
    return {
        "q": w_qkv[l, :, :WIDTH],
        "k": w_qkv[l, :, WIDTH : 2 * WIDTH],
        "vt": w_qkv[l, :, 2 * WIDTH :].T,
        "out": w_out[l],
        "up": w_up[l],
        "down": w_down[l],
        "gain": norm_attn[l : l + 1],
        "gain2": norm_mlp[l : l + 1],
    }


def shards(tokens, registers, tile_mask, w_qkv, w_out, w_up, w_down, norm_attn, norm_mlp):
    places = [(lax.axis_index(axis), lax.axis_size(axis)) for axis in ("row", "col")]
    flags = jnp.stack([f for at, n in places for f in (at > 0, at < n - 1)])
    flags = flags.astype(jnp.int32).reshape(1, 4)

    def rim(x, mask_row):
        live = jnp.repeat(mask_row, TILE)[None, :, None] > 0
        return to_groups(jnp.where(live, x, jnp.asarray(BIG, BF16)))

    first, last = rim(tokens[:REACH], tile_mask[0]), rim(tokens[-REACH:], tile_mask[-1])
    x, g = to_groups(tokens), registers
    for l in range(LAYERS):
        dil = DILATIONS[l % 2]
        w = layer_weights(l, w_qkv, w_out, w_up, w_down, norm_attn, norm_mlp)
        top, bottom = exchanged(first, last, "row")
        own, stats, left_own, right_own = own_tokens(dil, x, tile_mask, g, w)
        stats = joined(stats)
        left_own = jnp.concatenate([top[:, 0], left_own, bottom[:, 0]], axis=1)
        right_own = jnp.concatenate([top[:, -1], right_own, bottom[:, -1]], axis=1)
        left, right = exchanged(left_own, right_own, "col")
        rims = (top, bottom)
        middle = attend(dil, flags, tile_mask, x, own, rims, g, w)
        out = attend(dil, flags, tile_mask, x, own, rims, g, w, (left, right, middle))
        g = finish_registers(stats, g, w)
        if l < LAYERS - 1:
            x, first, last = out
    return out[0], g


def solution(mesh):
    return jax.shard_map(
        shards,
        mesh=mesh,
        in_specs=(P("row", "col", None), P(), P("row", "col"), P(), P(), P(), P(), P(), P()),
        out_specs=(P("row", "col", None), P()),
        check_vma=False,
    )
```
